256 devices in a mesh: pair: 8 (over y, z_lo), virt: 32 (over x, z_hi, core).
Axes of the slice: x: 4, y: 4, z: 8 (z_hi: 4, z_lo: 2; z = z_hi * 2 + z_lo), core: 2. Of those that a mesh axis runs over, the one named last changes fastest.
Arguments:
- amplitudes: bfloat16 [8192, 131072], P('pair', 'virt'), may hold values from -6 to 6
- integrals: bfloat16 [131072, 1024], P('virt', 'pair'), may hold values from -0.015625 to 0.015625
- occ_pairs: int32 [8192, 2], P(('pair', 'virt')), may hold values from 0 to 95, as said below
- partners: int32 [8192], P(('pair', 'virt')), may hold values from 0 to 8191, as said below
- virt_list: int32 [32], replicated, may hold values from 0 to 511
- eps_occ: float32 [96], replicated, may hold values from -2 to -0.5
- eps_virt: float32 [512], replicated, may hold values from 0.2 to 3
Outputs:
- update: float32 [8192, 1024], P(('pair', 'virt'))
The draws below stay inside these ranges and needn't reach their ends.
Inputs may be any that keep to these rules, and one draw needn't show every extreme that they name: Row r holds the pair (i, j) with i != j; row partners[r] holds (j, i), partners[partners[r]] = r, and partners[r] lies in the same index of pair and in the index of virt 32 / 2 away under the placement of the output rows. `occ_pairs`: the two orbitals of a row differ.
All inputs are finite; a program needn't handle non-finite values.
Results may differ from the reference program's by a relative error of at most 0.0003.
Values may be sent and summed in bfloat16 or wider, within the bound.
A program may use at most 192 MiB of HBM per device.

```python
import jax
import jax.numpy as jnp

NV = 512
NO = 96
W = 32
OP_DEV = 1024
CD = 131072
AB = 1024
OPAIRS = 8192
N_PAIR = 8
N_VIRT = 32


def pair_tables(key):
    base_key = jax.random.fold_in(key, 11)
    key_first, key_second, key_perm = jax.random.split(base_key, 3)
    rows = OP_DEV // N_VIRT
    half = N_VIRT // 2
    first = jax.random.randint(key_first, (N_PAIR, half, rows), 0, NO).astype(jnp.int32)
    second = ((first + jax.random.randint(key_second, (N_PAIR, half, rows), 1, NO)) % NO).astype(jnp.int32)
    sigma = jax.vmap(lambda s: jax.random.permutation(s, rows))(jax.random.split(key_perm, N_PAIR * half))
    sigma = sigma.reshape(N_PAIR, half, rows).astype(jnp.int32)
    inverse = jnp.argsort(sigma, axis=-1).astype(jnp.int32)
    high_first = jnp.take_along_axis(second, inverse, axis=-1)
    high_second = jnp.take_along_axis(first, inverse, axis=-1)
    low_pairs = jnp.stack([first, second], axis=-1)
    high_pairs = jnp.stack([high_first, high_second], axis=-1)
    occ = jnp.concatenate([low_pairs, high_pairs], axis=1).reshape(OPAIRS, 2)
    block_base = (jnp.arange(N_PAIR, dtype=jnp.int32) * OP_DEV)[:, None, None]
    low_virt = jnp.arange(half, dtype=jnp.int32)[None, :, None]
    low_partner = block_base + (low_virt + half) * rows + sigma
    high_partner = block_base + low_virt * rows + inverse
    partner = jnp.concatenate([low_partner, high_partner], axis=1).reshape(OPAIRS)
    return (occ.astype(jnp.int32), partner.astype(jnp.int32))


def draw_occ_pairs(key, part):
    return pair_tables(key)[0]


def draw_partners(key, part):
    return pair_tables(key)[1]


def set_ends(result, key, low, high):
    place = [jax.random.randint(jax.random.fold_in(key, axis), (), 0, length) for axis, length in enumerate(result.shape)]
    main_axis = result.shape.index(max(result.shape))
    next_to = place[:main_axis] + [(place[main_axis] + 1) % result.shape[main_axis]] + place[main_axis + 1:]
    return result.at[tuple(place)].set(low).at[tuple(next_to)].set(high)


def spiked(entries, key, source, target, blocks, factor):
    owner, partner = [(jnp.arange(entries.shape[dim]) // (entries.shape[dim] // blocks)).reshape([-1 if axis == dim else 1 for axis in range(entries.ndim)]) for dim in (source, target)]
    chosen = jax.random.permutation(key, blocks)[partner]
    strong = (owner == chosen) | (owner == (partner + blocks // 2) % blocks)
    return jnp.where(strong, factor * entries, entries)


def levels(rng, shape, cuts, least, high):
    loudness, own = 1.0, jax.random.fold_in(rng, 6)
    for position, blocks in cuts:
        draws = jnp.exp(jax.random.uniform(jax.random.fold_in(own, position), (blocks,), jnp.float32, least / len(cuts), high / len(cuts)))
        loudness = loudness * jnp.repeat(draws, shape[position] // blocks).reshape([-1 if axis == position else 1 for axis in range(len(shape))])
    return loudness


def bell_draw(rng, shape, deviation, limit, cuts=(), held_as=jnp.bfloat16):
    result = jax.random.normal(rng, shape, jnp.float32) * deviation
    if len(cuts) > 0:
        result = levels(rng, shape, cuts, -0.22, 0.18) * result
    return jnp.clip(result, min=-limit, max=limit).astype(held_as)


def gaussian_with(own_key, dims, width, reach, pieces, heavy, held_as=jnp.bfloat16):
    result = width * jax.random.normal(own_key, dims, jnp.float32)
    if pieces:
        result = result * levels(own_key, dims, pieces, -0.22, 0.18)
    return jnp.clip(spiked(result, jax.random.fold_in(own_key, 3), *heavy), -reach, reach).astype(held_as)


def setup_inputs(seed: int = 0) -> dict:
    splits = jax.random.split(jax.random.key(seed), 8)
    return {
        "amplitudes": gaussian_with(splits[0], (OPAIRS, CD), 1.0, 6.0, ((0, 8), (1, 32)), (1, 0, 32, 2.75)),
        "integrals": bell_draw(splits[1], (CD, AB), CD ** -0.5, 0.015625, ((0, 32), (1, 8))),
        "occ_pairs": draw_occ_pairs(jax.random.fold_in(splits[7], 71), 0),
        "partners": draw_partners(jax.random.fold_in(splits[7], 71), 0),
        "virt_list": set_ends(jax.random.randint(splits[4], (W,), 0, NV), jax.random.fold_in(splits[4], 1), 0, NV - 1).astype(jnp.int32),
        "eps_occ": jnp.clip(jax.random.uniform(splits[5], (NO,), jnp.float32, -2.0, -0.5), -2.0, -0.5),
        "eps_virt": jnp.clip(jax.random.uniform(splits[6], (NV,), jnp.float32, 0.2, 3.0), 0.2, 3.0),
    }


def reference(amplitudes, integrals, occ_pairs, partners, virt_list, eps_occ, eps_virt):
    ladder = jnp.dot(amplitudes, integrals, preferred_element_type=jnp.float32)
    flipped = jnp.take(ladder, partners, axis=0)
    flipped = flipped.reshape(-1, W, W).transpose(0, 2, 1).reshape(-1, W * W)
    symmetric = ladder + flipped
    occ_sum = eps_occ[occ_pairs[:, 0]] + eps_occ[occ_pairs[:, 1]]
    virt_energy = eps_virt[virt_list]
    virt_sum = (virt_energy[:, None] + virt_energy[None, :]).reshape(-1)
    denominator = virt_sum[None, :] - occ_sum[:, None]
    return symmetric / denominator
```

```python
import functools

import jax
import jax.numpy as jnp
from jax import lax
from jax.experimental import pallas as pl
from jax.experimental.pallas import tpu as pltpu
from jax.sharding import PartitionSpec as P

F32 = jnp.float32
NY, NX, NH = 4, 4, 4
CHUNKS = 16
FIRST_Z = 10
GROUP = 256
MT = 256


def ladder_kernel(
    a_hbm, b_hbm, mine_ref, other_ref,
    a_v, b_v, c_v, r1_v, d_v, ra_v, rb_v, rc_v, rd_v, e_v, rz_v, m_v, o_v,
    a_sem, b_sem, ag_s, ag_r, s1_s, s1_r, sx_s, sx_r, sz_s, sz_r, so_s, so_r,
):
    nc, n1 = CHUNKS, FIRST_Z
    ch = b_v.shape[1]
    pair, virt = lax.axis_index("pair"), lax.axis_index("virt")
    y, z = pair // 2, pair % 2
    x, zh, core = virt // 8, (virt // 2) % 4, virt % 2

    def device(ny, nz, nx, nh, ncore):
        return {"pair": ny * 2 + nz, "virt": (nx * 4 + nh) * 2 + ncore}

    y_up, y_dn = (y + 1) % NY, (y + 3) % NY
    x_up, x_dn, x_far = (x + 1) % NX, (x + 3) % NX, (x + 2) % NX
    h_others = [(zh + 1) % NH, (zh + 3) % NH, (zh + 2) % NH]
    to_z = device(y, 1 - z, x, zh, core)
    to_up = device(y_up, z, x, zh, core)
    to_dn = device(y_dn, z, x, zh, core)
    to_core = device(y, z, x, zh, 1 - core)
    to_xu = device(y, z, x_up, zh, core)
    to_xd = device(y, z, x_dn, zh, core)
    to_xf = device(y, z, x_far, zh, core)
    to_h = [device(y, z, x, h, core) for h in h_others]
    partners = [to_z, to_up, to_dn, to_core, to_xu, to_xd, to_xf] + to_h

    b_copy = []
    for c in range(nc):
        cp = pltpu.make_async_copy(b_hbm.at[pl.ds(c * ch, ch)], b_v.at[z * nc + c], b_sem.at[c])
        cp.start()
        b_copy.append(cp)
    a_copy = []
    for c in range(nc):
        cp = pltpu.make_async_copy(a_hbm.at[:, pl.ds(c * ch, ch)], a_v.at[c], a_sem.at[c])
        cp.start()
        a_copy.append(cp)

    barrier = pltpu.get_barrier_semaphore()
    for dev in partners:
        pl.semaphore_signal(barrier, inc=1, device_id=dev, device_id_type=pl.DeviceIdType.MESH)
    pl.semaphore_wait(barrier, len(partners))

    def remote(src, dst, ssem, rsem, dev):
        return pltpu.make_async_remote_copy(
            src_ref=src, dst_ref=dst, send_sem=ssem, recv_sem=rsem,
            device_id=dev, device_id_type=pl.DeviceIdType.MESH,
        )

    def slot(s, rel, c):
        plane = z if rel == 0 else 1 - z
        return (s * 2 + plane) * nc + c

    def move(s_from, rel, s_to, rel_to, c, stream, dev):
        src = b_v.at[slot(s_from, rel, c)]
        dst = b_v.at[slot(s_to, rel, c)]
        remote(src, dst, ag_s.at[stream], ag_r.at[s_to * 2 + rel_to, c], dev).start()

    def send_z(s, c):
        move(s, 0, s, 1, c, 0, to_z)

    def send_up(rel, c):
        move(0, rel, 2, rel, c, 1, to_up)

    def send_dn(rel, c):
        move(0, rel, 1, rel, c, 2, to_dn)

    def relay_up(rel, c):
        move(2, rel, 3, rel, c, 1, to_up)

    def relay_dn(rel, c):
        move(1, rel, 3, rel, c, 2, to_dn)

    def arrived(s, rel, c):
        ref = b_v.at[slot(s, rel, c)]
        remote(ref, ref, ag_s.at[0], ag_r.at[s * 2 + rel, c], to_z).wait_recv()

    def multiply(slots, chunk0, count, first):
        rows = MT // 64

        def body(i, _):
            m = i % 4
            k = chunk0 + (i // 4) % count
            s = slots[0] + i // (4 * count)
            base = s * 2 * nc + k
            rhs = jnp.concatenate([b_v[base], b_v[base + nc]], axis=1)
            lhs = a_v[k, pl.ds(pl.multiple_of(m * MT, MT), MT), :]
            part = jnp.dot(lhs, rhs, preferred_element_type=F32).reshape(rows, 2, 32, GROUP)
            at = pl.ds(m * rows, rows)
            if first:
                c_v[s, at] = part
            else:
                c_v[s, at] = c_v[s, at] + part
            return 0

        lax.fori_loop(0, 4 * count * len(slots), body, 0)

    def r_core(g):
        return remote(c_v.at[g, :, 1 - core], r1_v.at[g], s1_s.at[g], s1_r.at[g], to_core)

    def r_x(g):
        return [
            remote(d_v.at[g, x_far, 0], ra_v.at[g], sx_s.at[g, 0], sx_r.at[g, 0], to_xu),
            remote(d_v.at[g, x_far, 1], rb_v.at[g], sx_s.at[g, 1], sx_r.at[g, 1], to_xd),
            remote(d_v.at[g, x_up, 1], rc_v.at[g, 1], sx_s.at[g, 2], sx_r.at[g, 2], to_xu),
            remote(d_v.at[g, x_dn, 0], rd_v.at[g, 0], sx_s.at[g, 3], sx_r.at[g, 3], to_xd),
            remote(d_v.at[g, x_up, 0], rc_v.at[g, 0], sx_s.at[g, 4], sx_r.at[g, 4], to_xu),
            remote(d_v.at[g, x_dn, 1], rd_v.at[g, 1], sx_s.at[g, 5], sx_r.at[g, 5], to_xd),
        ]

    def r_h(g):
        return [
            remote(e_v.at[g, h_others[k]], rz_v.at[g, k], sz_s.at[g, k], sz_r.at[g, k], to_h[k])
            for k in range(3)
        ]

    def r_far(g):
        return remote(m_v.at[g], o_v.at[g], so_s.at[g], so_r.at[g], to_xf)

    def stage1(g):
        r_core(g).start()

    def stage2(g):
        r_core(g).wait_recv()
        for xx in range(NX):
            rows = pl.ds(xx * NH, NH)
            total = c_v[g, rows, core] + r1_v[g, rows]
            d_v[g, xx, 0] = total[:, :, :128]
            d_v[g, xx, 1] = total[:, :, 128:]
        copies = r_x(g)
        for k in range(4):
            copies[k].start()

    def stage3(g):
        copies = r_x(g)
        copies[0].wait_recv()
        d_v[g, x_up, 0] = d_v[g, x_up, 0] + ra_v[g]
        copies[4].start()
        copies[1].wait_recv()
        d_v[g, x_dn, 1] = d_v[g, x_dn, 1] + rb_v[g]
        copies[5].start()

    def stage4(g):
        copies = r_x(g)
        for k in range(2, 6):
            copies[k].wait_recv()
        for half in range(2):
            e_v[g, :, half] = d_v[g, x, half] + rc_v[g, half] + rd_v[g, half]
        for cp in r_h(g):
            cp.start()

    def stage5(g):
        for cp in r_h(g):
            cp.wait_recv()
        m_v[g] = e_v[g, zh] + rz_v[g, 0] + rz_v[g, 1] + rz_v[g, 2]
        r_far(g).start()

    def stage6(g):
        r_far(g).wait_recv()
        owner = [y, y_up, y_dn, (y + 2) % NY][g]
        for half in range(2):
            cols = pl.ds(pl.multiple_of(owner * GROUP + half * 128, 128), 128)
            mine_ref[:, cols] = m_v[g, half]
            other_ref[:, cols] = o_v[g, half]

    stages = [stage1, stage2, stage3, stage4, stage5, stage6]

    for c in range(nc):
        b_copy[c].wait()
    for k in range(nc):
        send_z(0, k)
        late = (k + n1) % nc
        send_up(0, late)
        send_dn(0, late)
    for c in range(nc):
        a_copy[c].wait()

    for u in range(n1 // 2):
        if u < (nc - n1) // 2:
            lo, hi = n1 + 2 * u, n1 + 2 * u + 1
            for c in (lo, hi):
                arrived(1, 0, c)
                arrived(2, 0, c)
            relay_up(0, lo)
            relay_dn(0, hi)
            for c in (lo, hi):
                send_z(1, c)
                send_z(2, c)
        for c in (2 * u, 2 * u + 1):
            arrived(0, 1, c)
            send_up(1, c)
            send_dn(1, c)
        if u == 0:
            multiply([0], 0, 1, True)
            multiply([0], 1, 1, False)
        else:
            multiply([0], 2 * u, 2, False)

    for u in range(n1 // 2):
        lo, hi = 2 * u, 2 * u + 1
        for c in (lo, hi):
            arrived(1, 0, c)
            arrived(2, 0, c)
        relay_up(0, lo)
        relay_dn(0, hi)
    for c in range(n1, nc):
        arrived(0, 1, c)
    multiply([0], n1, nc - n1, False)
    stage1(0)

    for u in range(n1 // 2):
        if u < (nc - n1) // 2:
            for c in (n1 + 2 * u, n1 + 2 * u + 1):
                arrived(3, 0, c)
                send_z(3, c)
        lo, hi = 2 * u, 2 * u + 1
        for c in (lo, hi):
            arrived(1, 1, c)
            arrived(2, 1, c)
        relay_up(1, lo)
        relay_dn(1, hi)
        if u == 0:
            multiply([1, 2], 0, 1, True)
            multiply([1, 2], 1, 1, False)
        else:
            multiply([1, 2], lo, 2, False)
        stages[u + 1](0)
    for c in range(n1, nc):
        arrived(1, 1, c)
        arrived(2, 1, c)
    multiply([1, 2], n1, nc - n1, False)
    stage1(1)
    stage1(2)

    for c in range(n1, nc):
        arrived(3, 1, c)
    multiply([3], n1, 1, True)
    multiply([3], n1 + 1, nc - n1 - 1, False)
    for c in range(n1):
        arrived(3, 0, c)
        if c % 2 == 1 and c // 2 < 5:
            stages[c // 2 + 1](1)
            stages[c // 2 + 1](2)
    for c in range(n1):
        arrived(3, 1, c)
        multiply([3], c, 1, False)
    for stage in stages:
        stage(3)

    relays = (nc + n1) // 2
    for stream, count in ((0, nc + 3 * (nc - n1)), (1, nc + n1 + relays), (2, nc + n1 + relays)):
        ref = b_v.at[pl.ds(0, count)]
        remote(ref, ref, ag_s.at[stream], ag_r.at[0, 0], to_z).wait_send()
    for g in range(4):
        for cp in [r_core(g), r_far(g)] + r_x(g) + r_h(g):
            cp.wait_send()


def ladder_rows(amplitudes, integrals):
    rows, depth = amplitudes.shape
    ch = depth // CHUNKS
    vmem, dma = pltpu.VMEM, pltpu.SemaphoreType.DMA
    out = jax.ShapeDtypeStruct((32, 1024), F32)
    return pl.pallas_call(
        ladder_kernel,
        out_shape=(out, out),
        in_specs=[pl.BlockSpec(memory_space=pl.ANY)] * 2,
        out_specs=(pl.BlockSpec(memory_space=pltpu.VMEM),) * 2,
        scratch_shapes=[
            vmem((CHUNKS, rows, ch), jnp.bfloat16),
            vmem((8 * CHUNKS, ch, 128), jnp.bfloat16),
            vmem((4, 16, 2, 32, GROUP), F32),
            vmem((4, 16, 32, GROUP), F32),
            vmem((4, NX, 2, NH, 32, 128), F32),
            vmem((4, NH, 32, 128), F32),
            vmem((4, NH, 32, 128), F32),
            vmem((4, 2, NH, 32, 128), F32),
            vmem((4, 2, NH, 32, 128), F32),
            vmem((4, NH, 2, 32, 128), F32),
            vmem((4, 3, 2, 32, 128), F32),
            vmem((4, 2, 32, 128), F32),
            vmem((4, 2, 32, 128), F32),
            dma((CHUNKS,)),
            dma((CHUNKS,)),
            dma((3,)),
            dma((8, CHUNKS)),
            dma((4,)),
            dma((4,)),
            dma((4, 6)),
            dma((4, 6)),
            dma((4, 3)),
            dma((4, 3)),
            dma((4,)),
            dma((4,)),
        ],
        compiler_params=pltpu.CompilerParams(collective_id=0, has_side_effects=True, vmem_limit_bytes=48 << 20),
    )(amplitudes, integrals)


def transpose_block(values, width):
    count = values.shape[0]
    return values.reshape(count, width, width).transpose(0, 2, 1).reshape(count, width * width)


def per_device(amplitudes, integrals, occ_pairs, partners, virt_list, eps_occ, eps_virt):
    width = virt_list.shape[0]
    mine, other = ladder_rows(amplitudes, integrals)
    flipped = jnp.take(other, partners % mine.shape[0], axis=0)
    total = mine + transpose_block(flipped, width)
    occ_ids = jnp.arange(eps_occ.shape[0], dtype=jnp.int32)
    occ_match = occ_pairs[:, :, None] == occ_ids[None, None, :]
    occ_sum = jnp.sum(jnp.where(occ_match, eps_occ[None, None, :], 0.0), axis=(1, 2))
    virt_ids = jnp.arange(eps_virt.shape[0], dtype=jnp.int32)
    virt_match = virt_list[:, None] == virt_ids[None, :]
    virt_energy = jnp.sum(jnp.where(virt_match, eps_virt[None, :], 0.0), axis=1)
    virt_sum = (virt_energy[:, None] + virt_energy[None, :]).reshape(-1)
    denominator = virt_sum[None, :] - occ_sum[:, None]
    return total / denominator


def solution(mesh):
    placed = (
        P("pair", "virt"),
        P("virt", "pair"),
        P(("pair", "virt"), None),
        P(("pair", "virt")),
        P(),
        P(),
        P(),
    )
    return jax.shard_map(
        per_device, mesh=mesh, in_specs=placed, out_specs=P(("pair", "virt"), None), check_vma=False
    )
```

```python
import jax
import jax.numpy as jnp
from jax import lax
from jax.experimental import pallas as pl
from jax.experimental.pallas import tpu as pltpu
from jax.sharding import PartitionSpec as P

F32 = jnp.float32
NY, NX, NH = 4, 4, 4
CHUNKS = 16
FIRST_Z = 10


def ladder_kernel(
    a_hbm, b_hbm, mine_ref, other_ref,
    a_v, b_v, c_v, r1_v, d_v, ra_v, rb_v, rc_v, rd_v, e_v, rz_v, m_v, o_v,
    a_sem, b_sem, ag_s, ag_r, s1_s, s1_r, sx_s, sx_r, sz_s, sz_r, so_s, so_r,
):
    nc, n1 = CHUNKS, FIRST_Z
    ch = b_v.shape[1]
    pair, virt = lax.axis_index("pair"), lax.axis_index("virt")
    y, z = pair // 2, pair % 2
    x, zh, core = virt // 8, (virt // 2) % 4, virt % 2

    def device(ny, nz, nx, nh, ncore):
        return {"pair": ny * 2 + nz, "virt": (nx * 4 + nh) * 2 + ncore}

    y_up, y_dn = (y + 1) % NY, (y + 3) % NY
    x_up, x_dn, x_far = (x + 1) % NX, (x + 3) % NX, (x + 2) % NX
    h_others = [(zh + 1) % NH, (zh + 3) % NH, (zh + 2) % NH]
    to_z = device(y, 1 - z, x, zh, core)
    to_up = device(y_up, z, x, zh, core)
    to_dn = device(y_dn, z, x, zh, core)
    to_core = device(y, z, x, zh, 1 - core)
    to_xu = device(y, z, x_up, zh, core)
    to_xd = device(y, z, x_dn, zh, core)
    to_xf = device(y, z, x_far, zh, core)
    to_h = [device(y, z, x, h, core) for h in h_others]
    partners = [to_z, to_up, to_dn, to_core, to_xu, to_xd, to_xf] + to_h

    b_copy = []
    for c in range(nc):
        cp = pltpu.make_async_copy(b_hbm.at[pl.ds(c * ch, ch)], b_v.at[z * nc + c], b_sem.at[c])
        cp.start()
        b_copy.append(cp)
    a_copy = []
    for c in range(nc):
        cp = pltpu.make_async_copy(a_hbm.at[:, pl.ds(c * ch, ch)], a_v.at[c], a_sem.at[c])
        cp.start()
        a_copy.append(cp)

    barrier = pltpu.get_barrier_semaphore()
    for dev in partners:
        pl.semaphore_signal(barrier, inc=1, device_id=dev, device_id_type=pl.DeviceIdType.MESH)
    pl.semaphore_wait(barrier, len(partners))

    def remote(src, dst, ssem, rsem, dev):
        return pltpu.make_async_remote_copy(
            src_ref=src, dst_ref=dst, send_sem=ssem, recv_sem=rsem,
            device_id=dev, device_id_type=pl.DeviceIdType.MESH,
        )

    def slot(s, rel, c):
        plane = z if rel == 0 else 1 - z
        return (s * 2 + plane) * nc + c

    def move(s_from, rel, s_to, rel_to, c, stream, dev):
        src = b_v.at[slot(s_from, rel, c)]
        dst = b_v.at[slot(s_to, rel, c)]
        remote(src, dst, ag_s.at[stream], ag_r.at[s_to * 2 + rel_to, c], dev).start()

    def send_z(s, c):
        move(s, 0, s, 1, c, 0, to_z)

    def send_up(rel, c):
        move(0, rel, 2, rel, c, 1, to_up)

    def send_dn(rel, c):
        move(0, rel, 1, rel, c, 2, to_dn)

    def relay_up(rel, c):
        move(2, rel, 3, rel, c, 1, to_up)

    def relay_dn(rel, c):
        move(1, rel, 3, rel, c, 2, to_dn)

    def arrived(s, rel, c):
        ref = b_v.at[slot(s, rel, c)]
        remote(ref, ref, ag_s.at[0], ag_r.at[s * 2 + rel, c], to_z).wait_recv()

    blocks = [(0, 0), (0, 1), (1, 0), (2, 0), (1, 1), (2, 1), (3, 0), (3, 1)]
    sets = [(0, 2), (2, 2), (4, 2), (6, 1), (7, 1)]

    def multiply(j, chunk0, count, first=False):
        u0, n = sets[j]
        starts = [slot(s, rel, 0) for s, rel in blocks[u0:u0 + n]]

        def body(i, _):
            k = chunk0 + 2 * i
            lhs = jnp.concatenate([a_v[k], a_v[k + 1]], axis=1)
            rhs = [jnp.concatenate([b_v[start + k], b_v[start + k + 1]], axis=0) for start in starts]
            rhs = jnp.concatenate(rhs, axis=1) if n == 2 else rhs[0]
            part = jnp.dot(lhs, rhs, preferred_element_type=F32)
            for t in range(n):
                piece = part[:, t * 128:(t + 1) * 128].reshape(16, 2, 32, 128)
                c_v[u0 + t] = piece if first else c_v[u0 + t] + piece
            return 0

        lax.fori_loop(0, count // 2, body, 0)

    def r_core(j):
        at = pl.ds(*sets[j])
        return remote(c_v.at[at, :, 1 - core], r1_v.at[at], s1_s.at[j], s1_r.at[j], to_core)

    def r_x(j, k):
        at = pl.ds(*sets[j])
        lo, hi = pl.ds(0, 2), pl.ds(2, 2)
        src, dst, dev = [
            (d_v.at[at, x_far, lo], ra_v.at[at], to_xu),
            (d_v.at[at, x_far, hi], rb_v.at[at], to_xd),
            (d_v.at[at, x_up, hi], rc_v.at[at, hi], to_xu),
            (d_v.at[at, x_dn, lo], rd_v.at[at, lo], to_xd),
            (d_v.at[at, x_up, lo], rc_v.at[at, lo], to_xu),
            (d_v.at[at, x_dn, hi], rd_v.at[at, hi], to_xd),
        ][k]
        return remote(src, dst, sx_s.at[j, k], sx_r.at[j, k], dev)

    def r_h(j, k):
        at = pl.ds(*sets[j])
        return remote(e_v.at[at, h_others[k]], rz_v.at[k, at], sz_s.at[j, k], sz_r.at[j, k], to_h[k])

    def r_far(j):
        at = pl.ds(*sets[j])
        return remote(m_v.at[at], o_v.at[at], so_s.at[j], so_r.at[j], to_xf)

    def stage1(j):
        r_core(j).start()

    def stage2(j):
        r_core(j).wait_recv()
        at = pl.ds(*sets[j])
        for k, xx in enumerate((x_far, x_up, x_dn, x)):
            rows = pl.ds(xx * NH, NH)
            d_v[at, xx] = c_v[at, rows, core] + r1_v[at, rows]
            if k == 0:
                r_x(j, 0).start()
                r_x(j, 1).start()
            if k == 1:
                r_x(j, 2).start()
            if k == 2:
                r_x(j, 3).start()

    def stage3(j):
        at = pl.ds(*sets[j])
        lo, hi = pl.ds(0, 2), pl.ds(2, 2)
        r_x(j, 0).wait_recv()
        d_v[at, x_up, lo] = d_v[at, x_up, lo] + ra_v[at]
        r_x(j, 4).start()
        r_x(j, 1).wait_recv()
        d_v[at, x_dn, hi] = d_v[at, x_dn, hi] + rb_v[at]
        r_x(j, 5).start()

    def stage4(j):
        at = pl.ds(*sets[j])
        for k in range(2, 6):
            r_x(j, k).wait_recv()
        e_v[at] = d_v[at, x] + rc_v[at] + rd_v[at]
        for k in (2, 0, 1):
            r_h(j, k).start()

    def stage5(j):
        at = pl.ds(*sets[j])
        for k in range(3):
            r_h(j, k).wait_recv()
        m_v[at] = e_v[at, zh] + rz_v[0, at] + rz_v[1, at] + rz_v[2, at]
        r_far(j).start()

    def stage6(j):
        r_far(j).wait_recv()
        u0, n = sets[j]
        for u in range(u0, u0 + n):
            s, rel = blocks[u]
            owner = [y, y_up, y_dn, (y + 2) % NY][s] * 2 + (z if rel == 0 else 1 - z)
            cols = pl.ds(pl.multiple_of(owner * 128, 128), 128)
            mine_ref[:, cols] = m_v[u]
            other_ref[:, cols] = o_v[u]

    for c in range(nc):
        b_copy[c].wait()
    for k in range(nc):
        send_z(0, k)
        late = (k + n1) % nc
        send_up(0, late)
        send_dn(0, late)
    for c in range(nc):
        a_copy[c].wait()

    late_pairs = (nc - n1) // 2
    for u in range(n1 // 2):
        lo, hi = 2 * u, 2 * u + 1
        if u < late_pairs:
            for c in (n1 + lo, n1 + hi):
                arrived(1, 0, c)
                arrived(2, 0, c)
            relay_up(0, n1 + lo)
            relay_dn(0, n1 + hi)
            for c in (n1 + lo, n1 + hi):
                send_z(1, c)
                send_z(2, c)
        for c in (lo, hi):
            arrived(0, 1, c)
            send_up(1, c)
            send_dn(1, c)
        if u == 0:
            multiply(0, 0, 2, True)
            multiply(1, n1, 2, True)
        else:
            multiply(0, lo, 2)
            if u < late_pairs:
                multiply(1, n1 + lo, 2)

    for u in range(n1 // 2):
        lo, hi = 2 * u, 2 * u + 1
        for c in (lo, hi):
            arrived(1, 0, c)
            arrived(2, 0, c)
        relay_up(0, lo)
        relay_dn(0, hi)
        multiply(1, lo, 2)
        if u >= n1 // 2 - late_pairs:
            c = n1 + 2 * (u - n1 // 2 + late_pairs)
            arrived(0, 1, c)
            arrived(0, 1, c + 1)
            multiply(0, c, 2)
    stage1(0)
    stage1(1)

    for u in range(n1 // 2):
        lo, hi = 2 * u, 2 * u + 1
        if u < late_pairs:
            for c in (n1 + lo, n1 + hi):
                arrived(3, 0, c)
                send_z(3, c)
        for c in (lo, hi):
            arrived(1, 1, c)
            arrived(2, 1, c)
        relay_up(1, lo)
        relay_dn(1, hi)
        if u == 0:
            multiply(2, 0, 2, True)
            multiply(3, n1, 2, True)
        else:
            multiply(2, lo, 2)
            if u < late_pairs:
                multiply(3, n1 + lo, 2)
        if u < 3:
            stage = [stage2, stage3, stage4][u]
            stage(0)
            stage(1)
    for c in range(n1, nc):
        arrived(1, 1, c)
        arrived(2, 1, c)
    multiply(2, n1, nc - n1)
    stage1(2)

    for u in range(n1 // 2):
        lo, hi = 2 * u, 2 * u + 1
        arrived(3, 0, lo)
        arrived(3, 0, hi)
        multiply(3, lo, 2)
        if u == 2:
            stage2(2)
    stage1(3)
    for c in range(n1, nc):
        arrived(3, 1, c)
    multiply(4, n1, 2, True)
    multiply(4, n1 + 2, nc - n1 - 2)
    stage5(0)
    stage5(1)

    for u in range(n1 // 2):
        lo, hi = 2 * u, 2 * u + 1
        arrived(3, 1, lo)
        arrived(3, 1, hi)
        multiply(4, lo, 2)
        if u == 0:
            stage2(3)
        if u == 1:
            stage3(2)
        if u == 2:
            stage6(0)
            stage6(1)
        if u == 3:
            stage3(3)
    stage1(4)
    stage4(2)
    stage4(3)
    stage2(4)
    stage5(2)
    stage3(4)
    stage5(3)
    stage4(4)
    stage6(2)
    stage6(3)
    stage5(4)
    stage6(4)

    relays = (nc + n1) // 2
    for stream, count in ((0, nc + 3 * (nc - n1)), (1, nc + n1 + relays), (2, nc + n1 + relays)):
        ref = b_v.at[pl.ds(0, count)]
        remote(ref, ref, ag_s.at[stream], ag_r.at[0, 0], to_z).wait_send()
    for j in range(len(sets)):
        for cp in [r_core(j), r_far(j)] + [r_x(j, k) for k in range(6)] + [r_h(j, k) for k in range(3)]:
            cp.wait_send()


def ladder_rows(amplitudes, integrals):
    rows, depth = amplitudes.shape
    ch = depth // CHUNKS
    vmem, dma = pltpu.VMEM, pltpu.SemaphoreType.DMA
    out = jax.ShapeDtypeStruct((32, 1024), F32)
    return pl.pallas_call(
        ladder_kernel,
        out_shape=(out, out),
        in_specs=[pl.BlockSpec(memory_space=pl.ANY)] * 2,
        out_specs=(pl.BlockSpec(memory_space=pltpu.VMEM),) * 2,
        scratch_shapes=[
            vmem((CHUNKS, rows, ch), jnp.bfloat16),
            vmem((8 * CHUNKS, ch, 128), jnp.bfloat16),
            vmem((8, 16, 2, 32, 128), F32),
            vmem((8, 16, 32, 128), F32),
            vmem((8, NX, NH, 32, 128), F32),
            vmem((8, 2, 32, 128), F32),
            vmem((8, 2, 32, 128), F32),
            vmem((8, NH, 32, 128), F32),
            vmem((8, NH, 32, 128), F32),
            vmem((8, NH, 32, 128), F32),
            vmem((3, 8, 32, 128), F32),
            vmem((8, 32, 128), F32),
            vmem((8, 32, 128), F32),
            dma((CHUNKS,)),
            dma((CHUNKS,)),
            dma((3,)),
            dma((8, CHUNKS)),
            dma((5,)),
            dma((5,)),
            dma((5, 6)),
            dma((5, 6)),
            dma((5, 3)),
            dma((5, 3)),
            dma((5,)),
            dma((5,)),
        ],
        compiler_params=pltpu.CompilerParams(collective_id=0, has_side_effects=True, vmem_limit_bytes=48 << 20),
    )(amplitudes, integrals)


def transpose_block(values, width):
    count = values.shape[0]
    return values.reshape(count, width, width).transpose(0, 2, 1).reshape(count, width * width)


def per_device(amplitudes, integrals, occ_pairs, partners, virt_list, eps_occ, eps_virt):
    width = virt_list.shape[0]
    mine, other = ladder_rows(amplitudes, integrals)
    flipped = jnp.take(other, partners % mine.shape[0], axis=0)
    total = mine + transpose_block(flipped, width)
    occ_ids = jnp.arange(eps_occ.shape[0], dtype=jnp.int32)
    occ_match = occ_pairs[:, :, None] == occ_ids[None, None, :]
    occ_sum = jnp.sum(jnp.where(occ_match, eps_occ[None, None, :], 0.0), axis=(1, 2))
    virt_ids = jnp.arange(eps_virt.shape[0], dtype=jnp.int32)
    virt_match = virt_list[:, None] == virt_ids[None, :]
    virt_energy = jnp.sum(jnp.where(virt_match, eps_virt[None, :], 0.0), axis=1)
    virt_sum = (virt_energy[:, None] + virt_energy[None, :]).reshape(-1)
    denominator = virt_sum[None, :] - occ_sum[:, None]
    return total / denominator


def solution(mesh):
    placed = (
        P("pair", "virt"),
        P("virt", "pair"),
        P(("pair", "virt"), None),
        P(("pair", "virt")),
        P(),
        P(),
        P(),
    )
    return jax.shard_map(
        per_device, mesh=mesh, in_specs=placed, out_specs=P(("pair", "virt"), None), check_vma=False
    )
```

```python
import jax
import jax.numpy as jnp
from jax import lax
from jax.experimental import pallas as pl
from jax.experimental.pallas import tpu as pltpu
from jax.sharding import PartitionSpec as P

F32 = jnp.float32
NY, NX, NH = 4, 4, 4
CHUNKS = 16
FIRST_Z = 10


def ladder_kernel(
    a_hbm, b_hbm, mine_ref, other_ref,
    a_v, b_v, c_v, r1_v, d_v, rf_v, rc_v, rd_v, e_v, rz_v, m_v, o_v,
    a_sem, b_sem, ag_s, ag_r, s1_s, s1_r, sx_s, sx_r, sz_s, sz_r, so_s, so_r,
    z_known, x_known, h_known,
):
    nc, n1 = CHUNKS, FIRST_Z
    ch = b_v.shape[1]
    pair, virt = lax.axis_index("pair"), lax.axis_index("virt")
    y, z = pair // 2, pair % 2
    x, zh, core = virt // 8, (virt // 2) % 4, virt % 2

    def device(ny, nz, nx, nh, ncore):
        return {"pair": ny * 2 + nz, "virt": (nx * 4 + nh) * 2 + ncore}

    y_up, y_dn = (y + 1) % NY, (y + 3) % NY
    x_up, x_dn, x_far = (x + 1) % NX, (x + 3) % NX, (x + 2) % NX
    h_others = [(zh + 1) % NH, (zh + 3) % NH, (zh + 2) % NH]
    to_z = device(y, 1 - z, x, zh, core)
    to_up = device(y_up, z, x, zh, core)
    to_dn = device(y_dn, z, x, zh, core)
    to_core = device(y, z, x, zh, 1 - core)
    to_xu = device(y, z, x_up, zh, core)
    to_xd = device(y, z, x_dn, zh, core)
    to_xf = device(y, z, x_far, zh, core)
    to_h = [device(y, z, x, h, core) for h in h_others]
    to_zz = device(y, 1 - z, x, (zh + NH + 2 * z - 1) % NH, core)
    near = [to_z, to_zz, to_up, to_dn, to_core, to_xu, to_xd]

    barrier = pltpu.get_barrier_semaphore()

    def signal(sem, dev):
        pl.semaphore_signal(sem, inc=1, device_id=dev, device_id_type=pl.DeviceIdType.MESH)

    for dev in near:
        signal(barrier, dev)
    b_copy = []
    for c in range(nc):
        cp = pltpu.make_async_copy(b_hbm.at[pl.ds(c * ch, ch)], b_v.at[z * nc + c], b_sem.at[c])
        cp.start()
        b_copy.append(cp)
    pl.semaphore_wait(barrier, len(near))

    def remote(src, dst, ssem, rsem, dev):
        return pltpu.make_async_remote_copy(
            src_ref=src, dst_ref=dst, send_sem=ssem, recv_sem=rsem,
            device_id=dev, device_id_type=pl.DeviceIdType.MESH,
        )

    def slot(s, rel, c):
        plane = z if rel == 0 else 1 - z
        return (s * 2 + plane) * nc + c

    def move(s_from, rel, s_to, rel_to, c, stream, dev):
        src = b_v.at[slot(s_from, rel, c)]
        dst = b_v.at[slot(s_to, rel, c)]
        remote(src, dst, ag_s.at[stream], ag_r.at[s_to * 2 + rel_to, c], dev).start()

    def send_z(s, c):
        move(s, 0, s, 1, c, 0, to_z)

    def send_up(rel, c):
        move(0, rel, 2, rel, c, 1, to_up)

    def send_dn(rel, c):
        move(0, rel, 1, rel, c, 2, to_dn)

    def relay_up(rel, c):
        move(2, rel, 3, rel, c, 1, to_up)

    def relay_dn(rel, c):
        move(1, rel, 3, rel, c, 2, to_dn)

    def arrived(s, rel, c):
        ref = b_v.at[slot(s, rel, c)]
        remote(ref, ref, ag_s.at[0], ag_r.at[s * 2 + rel, c], to_z).wait_recv()

    blocks = [(0, 0), (0, 1), (1, 0), (2, 0), (1, 1), (2, 1), (3, 0), (3, 1)]
    sets = [(0, 2), (2, 2), (4, 2), (6, 1), (7, 1)]

    def multiply(j, chunk0, count, first=False):
        u0, n = sets[j]
        starts = [slot(s, rel, 0) for s, rel in blocks[u0:u0 + n]]

        def body(i, _):
            k = chunk0 + 2 * i
            lhs = jnp.concatenate([a_v[k], a_v[k + 1]], axis=1)
            rhs = [jnp.concatenate([b_v[start + k], b_v[start + k + 1]], axis=0) for start in starts]
            rhs = jnp.concatenate(rhs, axis=1) if n == 2 else rhs[0]
            part = jnp.dot(lhs, rhs, preferred_element_type=F32)
            for t in range(n):
                piece = part[:, t * 128:(t + 1) * 128].reshape(16, 2, 32, 128)
                c_v[u0 + t] = piece if first else c_v[u0 + t] + piece
            return 0

        lax.fori_loop(0, count // 2, body, 0)

    x_order = [x_far, x_up, x_dn, x]

    def r_core(j, k):
        at, rows = pl.ds(*sets[j]), pl.ds(x_order[k] * NH, NH)
        return remote(c_v.at[at, rows, 1 - core], r1_v.at[at, rows], s1_s.at[j, k], s1_r.at[j, k], to_core)

    def r_x(j, k):
        at = pl.ds(*sets[j])
        dst, dev = [(rf_v, to_xf), (rc_v, to_xu), (rd_v, to_xd)][k]
        return remote(d_v.at[at, x_order[k]], dst.at[at], sx_s.at[j, k], sx_r.at[j, k], dev)

    def r_h(j, k):
        at = pl.ds(*sets[j])
        return remote(e_v.at[at, h_others[k]], rz_v.at[k, at], sz_s.at[j, k], sz_r.at[j, k], to_h[k])

    def r_far(j):
        at = pl.ds(*sets[j])
        return remote(m_v.at[at], o_v.at[at], so_s.at[j], so_r.at[j], to_xf)

    def stage1(j):
        for k in range(4):
            r_core(j, k).start()

    def stage2(j):
        at = pl.ds(*sets[j])
        for k, xx in enumerate(x_order):
            rows = pl.ds(xx * NH, NH)
            r_core(j, k).wait_recv()
            d_v[at, xx] = c_v[at, rows, core] + r1_v[at, rows]
            if k < 3:
                r_x(j, k).start()

    def stage3(j):
        at = pl.ds(*sets[j])
        for k in range(3):
            r_x(j, k).wait_recv()
        e_v[at] = d_v[at, x] + rc_v[at] + rd_v[at] + rf_v[at]
        for k in (2, 0, 1):
            r_h(j, k).start()

    def stage4(j):
        at = pl.ds(*sets[j])
        for k in range(3):
            r_h(j, k).wait_recv()
        m_v[at] = e_v[at, zh] + rz_v[0, at] + rz_v[1, at] + rz_v[2, at]
        r_far(j).start()

    def stage5(j):
        r_far(j).wait_recv()
        u0, n = sets[j]
        for u in range(u0, u0 + n):
            s, rel = blocks[u]
            owner = [y, y_up, y_dn, (y + 2) % NY][s] * 2 + (z if rel == 0 else 1 - z)
            cols = pl.ds(pl.multiple_of(owner * 128, 128), 128)
            mine_ref[:, cols] = m_v[u]
            other_ref[:, cols] = o_v[u]

    for c in range(nc):
        b_copy[c].wait()
    for k in range(nc):
        send_z(0, k)
        late = (k + n1) % nc
        send_up(0, late)
        send_dn(0, late)
    signal(z_known, to_z)
    signal(z_known, to_zz)
    signal(x_known, to_xu)
    signal(x_known, to_xd)
    a_copy = []
    for c in range(nc):
        cp = pltpu.make_async_copy(a_hbm.at[:, pl.ds(c * ch, ch)], a_v.at[c], a_sem.at[c])
        cp.start()
        a_copy.append(cp)
    for c in range(nc):
        a_copy[c].wait()
    pl.semaphore_wait(z_known, 2)
    signal(h_known, to_h[0])
    signal(h_known, to_h[1])

    late_pairs = (nc - n1) // 2
    for u in range(n1 // 2):
        lo, hi = 2 * u, 2 * u + 1
        if u < late_pairs:
            for c in (n1 + lo, n1 + hi):
                arrived(1, 0, c)
                arrived(2, 0, c)
            relay_up(0, n1 + lo)
            relay_dn(0, n1 + hi)
            for c in (n1 + lo, n1 + hi):
                send_z(1, c)
                send_z(2, c)
        for c in (lo, hi):
            arrived(0, 1, c)
            send_up(1, c)
            send_dn(1, c)
        if u == 0:
            multiply(0, 0, 2, True)
            multiply(1, n1, 2, True)
        else:
            multiply(0, lo, 2)
            if u < late_pairs:
                multiply(1, n1 + lo, 2)

    for u in range(n1 // 2):
        lo, hi = 2 * u, 2 * u + 1
        for c in (lo, hi):
            arrived(1, 0, c)
            arrived(2, 0, c)
        relay_up(0, lo)
        relay_dn(0, hi)
        multiply(1, lo, 2)
        if u >= n1 // 2 - late_pairs:
            c = n1 + 2 * (u - n1 // 2 + late_pairs)
            arrived(0, 1, c)
            arrived(0, 1, c + 1)
            multiply(0, c, 2)
    pl.semaphore_wait(x_known, 2)
    pl.semaphore_wait(h_known, 2)
    stage1(0)
    stage1(1)

    for u in range(n1 // 2):
        lo, hi = 2 * u, 2 * u + 1
        if u < late_pairs:
            for c in (n1 + lo, n1 + hi):
                arrived(3, 0, c)
                send_z(3, c)
        for c in (lo, hi):
            arrived(1, 1, c)
            arrived(2, 1, c)
        relay_up(1, lo)
        relay_dn(1, hi)
        if u == 0:
            multiply(2, 0, 2, True)
            multiply(3, n1, 2, True)
        else:
            multiply(2, lo, 2)
            if u < late_pairs:
                multiply(3, n1 + lo, 2)
        if u in (0, 3):
            stage = stage2 if u == 0 else stage3
            stage(0)
            stage(1)
    for c in range(n1, nc):
        arrived(1, 1, c)
        arrived(2, 1, c)
    multiply(2, n1, nc - n1)
    stage1(2)

    for u in range(n1 // 2):
        lo, hi = 2 * u, 2 * u + 1
        arrived(3, 0, lo)
        arrived(3, 0, hi)
        multiply(3, lo, 2)
        if u == 2:
            stage2(2)
    stage1(3)
    for c in range(n1, nc):
        arrived(3, 1, c)
    multiply(4, n1, 2, True)
    multiply(4, n1 + 2, nc - n1 - 2)

    for u in range(n1 // 2):
        lo, hi = 2 * u, 2 * u + 1
        arrived(3, 1, lo)
        arrived(3, 1, hi)
        multiply(4, lo, 2)
        if u == 0:
            stage2(3)
    stage1(4)
    stage2(4)
    stage3(2)
    stage3(3)
    stage3(4)
    stage4(0)
    stage4(1)
    stage4(2)
    stage4(3)
    stage4(4)
    stage5(0)
    stage5(1)
    stage5(2)
    stage5(3)
    stage5(4)

    relays = (nc + n1) // 2
    for stream, count in ((0, nc + 3 * (nc - n1)), (1, nc + n1 + relays), (2, nc + n1 + relays)):
        ref = b_v.at[pl.ds(0, count)]
        remote(ref, ref, ag_s.at[stream], ag_r.at[0, 0], to_z).wait_send()
    for j in range(len(sets)):
        for cp in [r_far(j)] + [r_core(j, k) for k in range(4)] + [r_x(j, k) for k in range(3)] + [r_h(j, k) for k in range(3)]:
            cp.wait_send()


def ladder_rows(amplitudes, integrals):
    rows, depth = amplitudes.shape
    ch = depth // CHUNKS
    vmem, dma = pltpu.VMEM, pltpu.SemaphoreType.DMA
    out = jax.ShapeDtypeStruct((32, 1024), F32)
    return pl.pallas_call(
        ladder_kernel,
        out_shape=(out, out),
        in_specs=[pl.BlockSpec(memory_space=pl.ANY)] * 2,
        out_specs=(pl.BlockSpec(memory_space=pltpu.VMEM),) * 2,
        scratch_shapes=[
            vmem((CHUNKS, rows, ch), jnp.bfloat16),
            vmem((8 * CHUNKS, ch, 128), jnp.bfloat16),
            vmem((8, 16, 2, 32, 128), F32),
            vmem((8, 16, 32, 128), F32),
            vmem((8, NX, NH, 32, 128), F32),
            vmem((8, NH, 32, 128), F32),
            vmem((8, NH, 32, 128), F32),
            vmem((8, NH, 32, 128), F32),
            vmem((8, NH, 32, 128), F32),
            vmem((3, 8, 32, 128), F32),
            vmem((8, 32, 128), F32),
            vmem((8, 32, 128), F32),
            dma((CHUNKS,)),
            dma((CHUNKS,)),
            dma((3,)),
            dma((8, CHUNKS)),
            dma((5, 4)),
            dma((5, 4)),
            dma((5, 3)),
            dma((5, 3)),
            dma((5, 3)),
            dma((5, 3)),
            dma((5,)),
            dma((5,)),
            pltpu.SemaphoreType.REGULAR,
            pltpu.SemaphoreType.REGULAR,
            pltpu.SemaphoreType.REGULAR,
        ],
        compiler_params=pltpu.CompilerParams(collective_id=0, has_side_effects=True, vmem_limit_bytes=63 << 20),
    )(amplitudes, integrals)


def transpose_block(values, width):
    count = values.shape[0]
    return values.reshape(count, width, width).transpose(0, 2, 1).reshape(count, width * width)


def per_device(amplitudes, integrals, occ_pairs, partners, virt_list, eps_occ, eps_virt):
    width = virt_list.shape[0]
    mine, other = ladder_rows(amplitudes, integrals)
    flipped = jnp.take(other, partners % mine.shape[0], axis=0)
    total = mine + transpose_block(flipped, width)
    occ_ids = jnp.arange(eps_occ.shape[0], dtype=jnp.int32)
    occ_match = occ_pairs[:, :, None] == occ_ids[None, None, :]
    occ_sum = jnp.sum(jnp.where(occ_match, eps_occ[None, None, :], 0.0), axis=(1, 2))
    virt_ids = jnp.arange(eps_virt.shape[0], dtype=jnp.int32)
    virt_match = virt_list[:, None] == virt_ids[None, :]
    virt_energy = jnp.sum(jnp.where(virt_match, eps_virt[None, :], 0.0), axis=1)
    virt_sum = (virt_energy[:, None] + virt_energy[None, :]).reshape(-1)
    denominator = virt_sum[None, :] - occ_sum[:, None]
    return total / denominator


def solution(mesh):
    placed = (
        P("pair", "virt"),
        P("virt", "pair"),
        P(("pair", "virt"), None),
        P(("pair", "virt")),
        P(),
        P(),
        P(),
    )
    return jax.shard_map(
        per_device, mesh=mesh, in_specs=placed, out_specs=P(("pair", "virt"), None), check_vma=False
    )
```

```python
import jax
import jax.numpy as jnp
from jax import lax
from jax.experimental import pallas as pl
from jax.experimental.pallas import tpu as pltpu
from jax.sharding import PartitionSpec as P

F32 = jnp.float32
NY, NX, NH = 4, 4, 4
CHUNKS = 16
FIRST_Z = 10
TOP = 32767.0
LIFT = 2.0 ** 60


def ladder_kernel(
    a_hbm, b_hbm, mine_ref, other_ref,
    a_v, b_v, c_v, r1_v, d_v, dq_v, ds_v, rq_v, rs_v, e_v, eq_v, es_v, rzq_v, rzs_v, m_v, o_v,
    a_sem, b_sem, ag_s, ag_r, s1_s, s1_r, sx_s, sx_r, sz_s, sz_r, so_s, so_r,
    z_known, x_known, h_known,
):
    nc, n1 = CHUNKS, FIRST_Z
    ch = b_v.shape[1]
    pair, virt = lax.axis_index("pair"), lax.axis_index("virt")
    y, z = pair // 2, pair % 2
    x, zh, core = virt // 8, (virt // 2) % 4, virt % 2

    def device(ny, nz, nx, nh, ncore):
        return {"pair": ny * 2 + nz, "virt": (nx * 4 + nh) * 2 + ncore}

    y_up, y_dn = (y + 1) % NY, (y + 3) % NY
    x_up, x_dn, x_far = (x + 1) % NX, (x + 3) % NX, (x + 2) % NX
    h_others = [(zh + 1) % NH, (zh + 3) % NH, (zh + 2) % NH]
    to_z = device(y, 1 - z, x, zh, core)
    to_up = device(y_up, z, x, zh, core)
    to_dn = device(y_dn, z, x, zh, core)
    to_core = device(y, z, x, zh, 1 - core)
    to_xu = device(y, z, x_up, zh, core)
    to_xd = device(y, z, x_dn, zh, core)
    to_xf = device(y, z, x_far, zh, core)
    to_h = [device(y, z, x, h, core) for h in h_others]
    to_zz = device(y, 1 - z, x, (zh + NH + 2 * z - 1) % NH, core)
    near = [to_z, to_zz, to_up, to_dn, to_core, to_xu, to_xd]

    barrier = pltpu.get_barrier_semaphore()

    def signal(sem, dev):
        pl.semaphore_signal(sem, inc=1, device_id=dev, device_id_type=pl.DeviceIdType.MESH)

    for dev in near:
        signal(barrier, dev)
    b_copy = []
    for c in range(nc):
        cp = pltpu.make_async_copy(b_hbm.at[pl.ds(c * ch, ch)], b_v.at[z * nc + c], b_sem.at[c])
        cp.start()
        b_copy.append(cp)
    pl.semaphore_wait(barrier, len(near))

    def remote(src, dst, ssem, rsem, dev):
        return pltpu.make_async_remote_copy(
            src_ref=src, dst_ref=dst, send_sem=ssem, recv_sem=rsem,
            device_id=dev, device_id_type=pl.DeviceIdType.MESH,
        )

    def slot(s, rel, c):
        plane = z if rel == 0 else 1 - z
        return (s * 2 + plane) * nc + c

    def move(s_from, rel, s_to, rel_to, c, stream, dev):
        src = b_v.at[slot(s_from, rel, c)]
        dst = b_v.at[slot(s_to, rel, c)]
        remote(src, dst, ag_s.at[stream], ag_r.at[s_to * 2 + rel_to, c], dev).start()

    def send_z(s, c):
        move(s, 0, s, 1, c, 0, to_z)

    def send_up(rel, c):
        move(0, rel, 2, rel, c, 1, to_up)

    def send_dn(rel, c):
        move(0, rel, 1, rel, c, 2, to_dn)

    def relay_up(rel, c):
        move(2, rel, 3, rel, c, 1, to_up)

    def relay_dn(rel, c):
        move(1, rel, 3, rel, c, 2, to_dn)

    def arrived(s, rel, c):
        ref = b_v.at[slot(s, rel, c)]
        remote(ref, ref, ag_s.at[0], ag_r.at[s * 2 + rel, c], to_z).wait_recv()

    blocks = [(0, 0), (0, 1), (1, 0), (2, 0), (1, 1), (2, 1), (3, 0), (3, 1)]
    sets = [(0, 2), (2, 2), (4, 2), (6, 1), (7, 1)]

    def multiply(j, chunk0, count, first=False):
        u0, n = sets[j]
        starts = [slot(s, rel, 0) for s, rel in blocks[u0:u0 + n]]

        def body(i, _):
            k = chunk0 + 2 * i
            lhs = jnp.concatenate([a_v[k], a_v[k + 1]], axis=1)
            rhs = [jnp.concatenate([b_v[start + k], b_v[start + k + 1]], axis=0) for start in starts]
            rhs = jnp.concatenate(rhs, axis=1) if n == 2 else rhs[0]
            part = jnp.dot(lhs, rhs, preferred_element_type=F32)
            for t in range(n):
                piece = part[:, t * 128:(t + 1) * 128].reshape(16, 2, 32, 128)
                c_v[u0 + t] = piece if first else c_v[u0 + t] + piece
            return 0

        lax.fori_loop(0, count // 2, body, 0)

    x_order = [x_far, x_up, x_dn, x]

    def r_core(j, k):
        at, rows = pl.ds(*sets[j]), pl.ds(x_order[k] * NH, NH)
        return remote(c_v.at[at, rows, 1 - core], r1_v.at[at, rows], s1_s.at[j, k], s1_r.at[j, k], to_core)

    def coded(value):
        most = jnp.max(jnp.abs(value), axis=2, keepdims=True)
        inverse = jnp.where(most > 0.0, TOP / jnp.maximum(most * LIFT, 1e-20), 0.0)
        level = jnp.floor((value * LIFT) * inverse + 0.5)
        return level.astype(jnp.int32).astype(jnp.int16), most * (1.0 / TOP)

    def decoded(level, scale):
        return level.astype(jnp.int32).astype(F32) * scale

    def r_x(j, k):
        at, dev = pl.ds(*sets[j]), [to_xf, to_xu, to_xd][k]
        return [
            remote(dq_v.at[k, at], rq_v.at[k, at], sx_s.at[j, k], sx_r.at[j, k], dev),
            remote(ds_v.at[k, at], rs_v.at[k, at], sx_s.at[j, 3 + k], sx_r.at[j, 3 + k], dev),
        ]

    def r_h(j, k):
        at = pl.ds(*sets[j])
        return [
            remote(eq_v.at[at, h_others[k]], rzq_v.at[k, at], sz_s.at[j, k], sz_r.at[j, k], to_h[k]),
            remote(es_v.at[at, h_others[k]], rzs_v.at[k, at], sz_s.at[j, 3 + k], sz_r.at[j, 3 + k], to_h[k]),
        ]

    def r_far(j):
        at = pl.ds(*sets[j])
        return remote(m_v.at[at], o_v.at[at], so_s.at[j], so_r.at[j], to_xf)

    def stage1(j):
        for k in range(4):
            r_core(j, k).start()

    def stage2(j):
        at = pl.ds(*sets[j])
        for k, xx in enumerate(x_order):
            rows = pl.ds(xx * NH, NH)
            r_core(j, k).wait_recv()
            total = c_v[at, rows, core] + r1_v[at, rows]
            if k == 3:
                d_v[at] = total
            else:
                dq_v[k, at], ds_v[k, at] = coded(total)
                for cp in r_x(j, k):
                    cp.start()

    def stage3(j):
        at = pl.ds(*sets[j])
        total = d_v[at]
        for k in (1, 2, 0):
            for cp in r_x(j, k):
                cp.wait_recv()
            total = total + decoded(rq_v[k, at], rs_v[k, at])
        e_v[at] = total
        eq_v[at], es_v[at] = coded(total)
        for k in (2, 0, 1):
            for cp in r_h(j, k):
                cp.start()

    def stage4(j):
        at = pl.ds(*sets[j])
        total = e_v[at, zh]
        for k in range(3):
            for cp in r_h(j, k):
                cp.wait_recv()
            total = total + decoded(rzq_v[k, at], rzs_v[k, at])
        m_v[at] = total
        r_far(j).start()

    def stage5(j):
        r_far(j).wait_recv()
        u0, n = sets[j]
        for u in range(u0, u0 + n):
            s, rel = blocks[u]
            owner = [y, y_up, y_dn, (y + 2) % NY][s] * 2 + (z if rel == 0 else 1 - z)
            cols = pl.ds(pl.multiple_of(owner * 128, 128), 128)
            mine_ref[:, cols] = m_v[u]
            other_ref[:, cols] = o_v[u]

    for c in range(nc):
        b_copy[c].wait()
    for k in range(nc):
        send_z(0, k)
        late = (k + n1) % nc
        send_up(0, late)
        send_dn(0, late)
    signal(z_known, to_z)
    signal(z_known, to_zz)
    signal(x_known, to_xu)
    signal(x_known, to_xd)
    a_copy = []
    for c in range(nc):
        cp = pltpu.make_async_copy(a_hbm.at[:, pl.ds(c * ch, ch)], a_v.at[c], a_sem.at[c])
        cp.start()
        a_copy.append(cp)
    for c in range(nc):
        a_copy[c].wait()
    pl.semaphore_wait(z_known, 2)
    signal(h_known, to_h[0])
    signal(h_known, to_h[1])

    late_pairs = (nc - n1) // 2
    for u in range(n1 // 2):
        lo, hi = 2 * u, 2 * u + 1
        if u < late_pairs:
            for c in (n1 + lo, n1 + hi):
                arrived(1, 0, c)
                arrived(2, 0, c)
            relay_up(0, n1 + lo)
            relay_dn(0, n1 + hi)
            for c in (n1 + lo, n1 + hi):
                send_z(1, c)
                send_z(2, c)
        for c in (lo, hi):
            arrived(0, 1, c)
            send_up(1, c)
            send_dn(1, c)
        if u == 0:
            multiply(0, 0, 2, True)
            multiply(1, n1, 2, True)
        else:
            multiply(0, lo, 2)
            if u < late_pairs:
                multiply(1, n1 + lo, 2)

    for u in range(n1 // 2):
        lo, hi = 2 * u, 2 * u + 1
        for c in (lo, hi):
            arrived(1, 0, c)
            arrived(2, 0, c)
        relay_up(0, lo)
        relay_dn(0, hi)
        multiply(1, lo, 2)
        if u >= n1 // 2 - late_pairs:
            c = n1 + 2 * (u - n1 // 2 + late_pairs)
            arrived(0, 1, c)
            arrived(0, 1, c + 1)
            multiply(0, c, 2)
    pl.semaphore_wait(x_known, 2)
    pl.semaphore_wait(h_known, 2)
    stage1(0)
    stage1(1)

    for u in range(n1 // 2):
        lo, hi = 2 * u, 2 * u + 1
        if u < late_pairs:
            for c in (n1 + lo, n1 + hi):
                arrived(3, 0, c)
                send_z(3, c)
        for c in (lo, hi):
            arrived(1, 1, c)
            arrived(2, 1, c)
        relay_up(1, lo)
        relay_dn(1, hi)
        if u == 0:
            multiply(2, 0, 2, True)
            multiply(3, n1, 2, True)
        else:
            multiply(2, lo, 2)
            if u < late_pairs:
                multiply(3, n1 + lo, 2)
        if u in (0, 3):
            stage = stage2 if u == 0 else stage3
            stage(0)
            stage(1)
    for c in range(n1, nc):
        arrived(1, 1, c)
        arrived(2, 1, c)
    multiply(2, n1, nc - n1)
    stage1(2)

    for u in range(n1 // 2):
        lo, hi = 2 * u, 2 * u + 1
        arrived(3, 0, lo)
        arrived(3, 0, hi)
        multiply(3, lo, 2)
        if u == 2:
            stage2(2)
    stage1(3)
    for c in range(n1, nc):
        arrived(3, 1, c)
    multiply(4, n1, 2, True)
    multiply(4, n1 + 2, nc - n1 - 2)

    for u in range(n1 // 2):
        lo, hi = 2 * u, 2 * u + 1
        arrived(3, 1, lo)
        arrived(3, 1, hi)
        multiply(4, lo, 2)
        if u == 0:
            stage2(3)
    stage1(4)
    stage2(4)
    stage3(2)
    stage3(3)
    stage3(4)
    stage4(0)
    stage4(1)
    stage4(2)
    stage4(3)
    stage4(4)
    stage5(0)
    stage5(1)
    stage5(2)
    stage5(3)
    stage5(4)

    relays = (nc + n1) // 2
    for stream, count in ((0, nc + 3 * (nc - n1)), (1, nc + n1 + relays), (2, nc + n1 + relays)):
        ref = b_v.at[pl.ds(0, count)]
        remote(ref, ref, ag_s.at[stream], ag_r.at[0, 0], to_z).wait_send()
    for j in range(len(sets)):
        r_far(j).wait_send()
        for k in range(4):
            r_core(j, k).wait_send()
        for k in range(3):
            for cp in r_x(j, k) + r_h(j, k):
                cp.wait_send()


def ladder_rows(amplitudes, integrals):
    rows, depth = amplitudes.shape
    ch = depth // CHUNKS
    vmem, dma = pltpu.VMEM, pltpu.SemaphoreType.DMA
    out = jax.ShapeDtypeStruct((32, 1024), F32)
    return pl.pallas_call(
        ladder_kernel,
        out_shape=(out, out),
        in_specs=[pl.BlockSpec(memory_space=pl.ANY)] * 2,
        out_specs=(pl.BlockSpec(memory_space=pltpu.VMEM),) * 2,
        scratch_shapes=[
            vmem((CHUNKS, rows, ch), jnp.bfloat16),
            vmem((8 * CHUNKS, ch, 128), jnp.bfloat16),
            vmem((8, 16, 2, 32, 128), F32),
            vmem((8, 16, 32, 128), F32),
            vmem((8, NH, 32, 128), F32),
            vmem((3, 8, NH, 32, 128), jnp.int16),
            vmem((3, 8, NH, 1, 128), F32),
            vmem((3, 8, NH, 32, 128), jnp.int16),
            vmem((3, 8, NH, 1, 128), F32),
            vmem((8, NH, 32, 128), F32),
            vmem((8, NH, 32, 128), jnp.int16),
            vmem((8, NH, 1, 128), F32),
            vmem((3, 8, 32, 128), jnp.int16),
            vmem((3, 8, 1, 128), F32),
            vmem((8, 32, 128), F32),
            vmem((8, 32, 128), F32),
            dma((CHUNKS,)),
            dma((CHUNKS,)),
            dma((3,)),
            dma((8, CHUNKS)),
            dma((5, 4)),
            dma((5, 4)),
            dma((5, 6)),
            dma((5, 6)),
            dma((5, 6)),
            dma((5, 6)),
            dma((5,)),
            dma((5,)),
            pltpu.SemaphoreType.REGULAR,
            pltpu.SemaphoreType.REGULAR,
            pltpu.SemaphoreType.REGULAR,
        ],
        compiler_params=pltpu.CompilerParams(collective_id=0, has_side_effects=True, vmem_limit_bytes=63 << 20),
    )(amplitudes, integrals)


def transpose_block(values, width):
    count = values.shape[0]
    return values.reshape(count, width, width).transpose(0, 2, 1).reshape(count, width * width)


def per_device(amplitudes, integrals, occ_pairs, partners, virt_list, eps_occ, eps_virt):
    width = virt_list.shape[0]
    mine, other = ladder_rows(amplitudes, integrals)
    flipped = jnp.take(other, partners % mine.shape[0], axis=0)
    total = mine + transpose_block(flipped, width)
    occ_ids = jnp.arange(eps_occ.shape[0], dtype=jnp.int32)
    occ_match = occ_pairs[:, :, None] == occ_ids[None, None, :]
    occ_sum = jnp.sum(jnp.where(occ_match, eps_occ[None, None, :], 0.0), axis=(1, 2))
    virt_ids = jnp.arange(eps_virt.shape[0], dtype=jnp.int32)
    virt_match = virt_list[:, None] == virt_ids[None, :]
    virt_energy = jnp.sum(jnp.where(virt_match, eps_virt[None, :], 0.0), axis=1)
    virt_sum = (virt_energy[:, None] + virt_energy[None, :]).reshape(-1)
    denominator = virt_sum[None, :] - occ_sum[:, None]
    return total / denominator


def solution(mesh):
    placed = (
        P("pair", "virt"),
        P("virt", "pair"),
        P(("pair", "virt"), None),
        P(("pair", "virt")),
        P(),
        P(),
        P(),
    )
    return jax.shard_map(
        per_device, mesh=mesh, in_specs=placed, out_specs=P(("pair", "virt"), None), check_vma=False
    )
```

```python
import jax
import jax.numpy as jnp
from jax import lax
from jax.experimental import pallas as pl
from jax.experimental.pallas import tpu as pltpu
from jax.sharding import PartitionSpec as P

F32 = jnp.float32
NY, NX, NH = 4, 4, 4
CHUNKS = 16
FIRST_Z = 10
TOP = 32767.0
LIFT = 2.0 ** 60


def ladder_kernel(
    a_hbm, b_hbm, mine_ref, other_ref,
    a_v, b_v, c_v, r1_v, d_v, dq_v, ds_v, rq_v, rs_v, e_v, eq_v, es_v, rzq_v, rzs_v, m_v, o_v,
    a_sem, b_sem, ag_s, ag_r, s1_s, s1_r, sx_s, sx_r, sz_s, sz_r, so_s, so_r,
    z_known, x_known, h_known,
):
    nc, n1 = CHUNKS, FIRST_Z
    ch = b_v.shape[1]
    pair, virt = lax.axis_index("pair"), lax.axis_index("virt")
    y, z = pair // 2, pair % 2
    x, zh, core = virt // 8, (virt // 2) % 4, virt % 2

    def device(ny, nz, nx, nh, ncore):
        return {"pair": ny * 2 + nz, "virt": (nx * 4 + nh) * 2 + ncore}

    y_up, y_dn = (y + 1) % NY, (y + 3) % NY
    x_up, x_dn, x_far = (x + 1) % NX, (x + 3) % NX, (x + 2) % NX
    h_others = [(zh + 1) % NH, (zh + 3) % NH, (zh + 2) % NH]
    to_z = device(y, 1 - z, x, zh, core)
    to_up = device(y_up, z, x, zh, core)
    to_dn = device(y_dn, z, x, zh, core)
    to_core = device(y, z, x, zh, 1 - core)
    to_xu = device(y, z, x_up, zh, core)
    to_xd = device(y, z, x_dn, zh, core)
    to_xf = device(y, z, x_far, zh, core)
    to_h = [device(y, z, x, h, core) for h in h_others]
    to_zz = device(y, 1 - z, x, (zh + NH + 2 * z - 1) % NH, core)
    near = [to_z, to_zz, to_up, to_dn, to_core, to_xu, to_xd]

    barrier = pltpu.get_barrier_semaphore()

    def signal(sem, dev):
        pl.semaphore_signal(sem, inc=1, device_id=dev, device_id_type=pl.DeviceIdType.MESH)

    for dev in near:
        signal(barrier, dev)
    b_copy = []
    for c in range(nc):
        cp = pltpu.make_async_copy(b_hbm.at[pl.ds(c * ch, ch)], b_v.at[z * nc + c], b_sem.at[c])
        cp.start()
        b_copy.append(cp)
    pl.semaphore_wait(barrier, len(near))

    def remote(src, dst, ssem, rsem, dev):
        return pltpu.make_async_remote_copy(
            src_ref=src, dst_ref=dst, send_sem=ssem, recv_sem=rsem,
            device_id=dev, device_id_type=pl.DeviceIdType.MESH,
        )

    def slot(s, rel, c):
        plane = z if rel == 0 else 1 - z
        return (s * 2 + plane) * nc + c

    def move(s_from, rel, s_to, rel_to, c, stream, dev):
        src = b_v.at[slot(s_from, rel, c)]
        dst = b_v.at[slot(s_to, rel, c)]
        remote(src, dst, ag_s.at[stream], ag_r.at[s_to * 2 + rel_to, c], dev).start()

    def send_z(s, c):
        move(s, 0, s, 1, c, 0, to_z)

    def send_up(rel, c):
        move(0, rel, 2, rel, c, 1, to_up)

    def send_dn(rel, c):
        move(0, rel, 1, rel, c, 2, to_dn)

    def relay_up(rel, c):
        move(2, rel, 3, rel, c, 1, to_up)

    def relay_dn(rel, c):
        move(1, rel, 3, rel, c, 2, to_dn)

    def arrived(s, rel, c):
        ref = b_v.at[slot(s, rel, c)]
        remote(ref, ref, ag_s.at[0], ag_r.at[s * 2 + rel, c], to_z).wait_recv()

    blocks = [(0, 0), (0, 1), (1, 0), (2, 0), (1, 1), (2, 1), (3, 0), (3, 1)]
    sets = [(0, 2), (2, 2), (4, 2), (6, 1), (7, 1)]

    def multiply(j, chunk0, count, first=False):
        u0, n = sets[j]
        starts = [slot(s, rel, 0) for s, rel in blocks[u0:u0 + n]]

        def body(i, _):
            k = chunk0 + 2 * i
            lhs = jnp.concatenate([a_v[k], a_v[k + 1]], axis=1)
            rhs = [jnp.concatenate([b_v[start + k], b_v[start + k + 1]], axis=0) for start in starts]
            rhs = jnp.concatenate(rhs, axis=1) if n == 2 else rhs[0]
            part = jnp.dot(lhs, rhs, preferred_element_type=F32)
            for t in range(n):
                piece = part[:, t * 128:(t + 1) * 128].reshape(16, 2, 32, 128)
                c_v[u0 + t] = piece if first else c_v[u0 + t] + piece
            return 0

        lax.fori_loop(0, count // 2, body, 0)

    x_order = [x_far, x_up, x_dn, x]

    def r_core(j, k):
        at, rows = pl.ds(*sets[j]), pl.ds(x_order[k] * NH, NH)
        return remote(c_v.at[at, rows, 1 - core], r1_v.at[at, rows], s1_s.at[j, k], s1_r.at[j, k], to_core)

    def coded(value):
        most = jnp.max(jnp.abs(value), axis=2, keepdims=True)
        inverse = jnp.where(most > 0.0, TOP / jnp.maximum(most * LIFT, 1e-20), 0.0)
        level = jnp.floor((value * LIFT) * inverse + 0.5)
        return level.astype(jnp.int32).astype(jnp.int16), most * (1.0 / TOP)

    def decoded(level, scale):
        return level.astype(jnp.int32).astype(F32) * scale

    def r_x(j, k):
        at, dev = pl.ds(*sets[j]), [to_xf, to_xu, to_xd][k]
        return [
            remote(dq_v.at[k, at], rq_v.at[k, at], sx_s.at[j, k], sx_r.at[j, k], dev),
            remote(ds_v.at[k, at], rs_v.at[k, at], sx_s.at[j, 3 + k], sx_r.at[j, 3 + k], dev),
        ]

    def r_h(j, k):
        at = pl.ds(*sets[j])
        return [
            remote(eq_v.at[at, h_others[k]], rzq_v.at[k, at], sz_s.at[j, k], sz_r.at[j, k], to_h[k]),
            remote(es_v.at[at, h_others[k]], rzs_v.at[k, at], sz_s.at[j, 3 + k], sz_r.at[j, 3 + k], to_h[k]),
        ]

    def r_far(j):
        at = pl.ds(*sets[j])
        return remote(m_v.at[at], o_v.at[at], so_s.at[j], so_r.at[j], to_xf)

    def stage1(j):
        for k in range(4):
            r_core(j, k).start()

    def stage2(j):
        at = pl.ds(*sets[j])
        for k, xx in enumerate(x_order):
            rows = pl.ds(xx * NH, NH)
            r_core(j, k).wait_recv()
            total = c_v[at, rows, core] + r1_v[at, rows]
            if k == 3:
                d_v[at] = total
            else:
                dq_v[k, at], ds_v[k, at] = coded(total)
                for cp in r_x(j, k):
                    cp.start()

    def stage3(j):
        at = pl.ds(*sets[j])
        total = d_v[at]
        for k in (1, 2, 0):
            for cp in r_x(j, k):
                cp.wait_recv()
            total = total + decoded(rq_v[k, at], rs_v[k, at])
        e_v[at] = total
        for k in (2, 0, 1):
            piece = pl.ds(h_others[k], 1)
            eq_v[at, piece], es_v[at, piece] = coded(e_v[at, piece])
            for cp in r_h(j, k):
                cp.start()

    def stage4(j):
        at = pl.ds(*sets[j])
        total = e_v[at, zh]
        for k in range(3):
            for cp in r_h(j, k):
                cp.wait_recv()
            total = total + decoded(rzq_v[k, at], rzs_v[k, at])
        m_v[at] = total
        r_far(j).start()

    def stage5(j):
        r_far(j).wait_recv()
        u0, n = sets[j]
        for u in range(u0, u0 + n):
            s, rel = blocks[u]
            owner = [y, y_up, y_dn, (y + 2) % NY][s] * 2 + (z if rel == 0 else 1 - z)
            cols = pl.ds(pl.multiple_of(owner * 128, 128), 128)
            mine_ref[:, cols] = m_v[u]
            other_ref[:, cols] = o_v[u]

    for c in range(nc):
        b_copy[c].wait()
    for k in range(nc):
        send_z(0, k)
        late = (k + n1) % nc
        send_up(0, late)
        send_dn(0, late)
    signal(z_known, to_z)
    signal(z_known, to_zz)
    signal(x_known, to_xu)
    signal(x_known, to_xd)
    a_copy = []
    for c in range(nc):
        cp = pltpu.make_async_copy(a_hbm.at[:, pl.ds(c * ch, ch)], a_v.at[c], a_sem.at[c])
        cp.start()
        a_copy.append(cp)
    for c in range(nc):
        a_copy[c].wait()
    pl.semaphore_wait(z_known, 2)
    signal(h_known, to_h[0])
    signal(h_known, to_h[1])

    late_pairs = (nc - n1) // 2
    for u in range(n1 // 2):
        lo, hi = 2 * u, 2 * u + 1
        if u < late_pairs:
            for c in (n1 + lo, n1 + hi):
                arrived(1, 0, c)
                arrived(2, 0, c)
            relay_up(0, n1 + lo)
            relay_dn(0, n1 + hi)
            for c in (n1 + lo, n1 + hi):
                send_z(1, c)
                send_z(2, c)
        for c in (lo, hi):
            arrived(0, 1, c)
            send_up(1, c)
            send_dn(1, c)
        if u == 0:
            multiply(0, 0, 2, True)
            multiply(1, n1, 2, True)
        else:
            multiply(0, lo, 2)
            if u < late_pairs:
                multiply(1, n1 + lo, 2)

    for u in range(n1 // 2):
        lo, hi = 2 * u, 2 * u + 1
        for c in (lo, hi):
            arrived(1, 0, c)
            arrived(2, 0, c)
        relay_up(0, lo)
        relay_dn(0, hi)
        multiply(1, lo, 2)
        if u >= n1 // 2 - late_pairs:
            c = n1 + 2 * (u - n1 // 2 + late_pairs)
            arrived(0, 1, c)
            arrived(0, 1, c + 1)
            multiply(0, c, 2)
    pl.semaphore_wait(x_known, 2)
    pl.semaphore_wait(h_known, 2)
    stage1(0)
    stage1(1)

    for u in range(n1 // 2):
        lo, hi = 2 * u, 2 * u + 1
        if u < late_pairs:
            for c in (n1 + lo, n1 + hi):
                arrived(3, 0, c)
                send_z(3, c)
        for c in (lo, hi):
            arrived(1, 1, c)
            arrived(2, 1, c)
        relay_up(1, lo)
        relay_dn(1, hi)
        if u == 0:
            multiply(2, 0, 2, True)
            multiply(3, n1, 2, True)
        else:
            multiply(2, lo, 2)
            if u < late_pairs:
                multiply(3, n1 + lo, 2)
        if u in (0, 3):
            stage = stage2 if u == 0 else stage3
            stage(0)
            stage(1)
    for c in range(n1, nc):
        arrived(1, 1, c)
        arrived(2, 1, c)
    multiply(2, n1, nc - n1)
    stage1(2)

    for u in range(n1 // 2):
        lo, hi = 2 * u, 2 * u + 1
        arrived(3, 0, lo)
        arrived(3, 0, hi)
        multiply(3, lo, 2)
        if u == 2:
            stage2(2)
    stage1(3)
    for c in range(n1, nc):
        arrived(3, 1, c)
    multiply(4, n1, 2, True)
    multiply(4, n1 + 2, nc - n1 - 2)

    for u in range(n1 // 2):
        lo, hi = 2 * u, 2 * u + 1
        arrived(3, 1, lo)
        arrived(3, 1, hi)
        multiply(4, lo, 2)
        if u == 0:
            stage2(3)
    stage1(4)
    stage2(4)
    stage3(2)
    stage3(3)
    stage3(4)
    stage4(0)
    stage4(1)
    stage4(2)
    stage4(3)
    stage4(4)
    stage5(0)
    stage5(1)
    stage5(2)
    stage5(3)
    relays = (nc + n1) // 2
    for stream, count in ((0, nc + 3 * (nc - n1)), (1, nc + n1 + relays), (2, nc + n1 + relays)):
        ref = b_v.at[pl.ds(0, count)]
        remote(ref, ref, ag_s.at[stream], ag_r.at[0, 0], to_z).wait_send()
    for j in range(len(sets)):
        r_far(j).wait_send()
        for k in range(4):
            r_core(j, k).wait_send()
        for k in range(3):
            for cp in r_x(j, k) + r_h(j, k):
                cp.wait_send()

    stage5(4)


def ladder_rows(amplitudes, integrals):
    rows, depth = amplitudes.shape
    ch = depth // CHUNKS
    vmem, dma = pltpu.VMEM, pltpu.SemaphoreType.DMA
    out = jax.ShapeDtypeStruct((32, 1024), F32)
    return pl.pallas_call(
        ladder_kernel,
        out_shape=(out, out),
        in_specs=[pl.BlockSpec(memory_space=pl.ANY)] * 2,
        out_specs=(pl.BlockSpec(memory_space=pltpu.VMEM),) * 2,
        scratch_shapes=[
            vmem((CHUNKS, rows, ch), jnp.bfloat16),
            vmem((8 * CHUNKS, ch, 128), jnp.bfloat16),
            vmem((8, 16, 2, 32, 128), F32),
            vmem((8, 16, 32, 128), F32),
            vmem((8, NH, 32, 128), F32),
            vmem((3, 8, NH, 32, 128), jnp.int16),
            vmem((3, 8, NH, 1, 128), F32),
            vmem((3, 8, NH, 32, 128), jnp.int16),
            vmem((3, 8, NH, 1, 128), F32),
            vmem((8, NH, 32, 128), F32),
            vmem((8, NH, 32, 128), jnp.int16),
            vmem((8, NH, 1, 128), F32),
            vmem((3, 8, 32, 128), jnp.int16),
            vmem((3, 8, 1, 128), F32),
            vmem((8, 32, 128), F32),
            vmem((8, 32, 128), F32),
            dma((CHUNKS,)),
            dma((CHUNKS,)),
            dma((3,)),
            dma((8, CHUNKS)),
            dma((5, 4)),
            dma((5, 4)),
            dma((5, 6)),
            dma((5, 6)),
            dma((5, 6)),
            dma((5, 6)),
            dma((5,)),
            dma((5,)),
            pltpu.SemaphoreType.REGULAR,
            pltpu.SemaphoreType.REGULAR,
            pltpu.SemaphoreType.REGULAR,
        ],
        compiler_params=pltpu.CompilerParams(collective_id=0, has_side_effects=True, vmem_limit_bytes=63 << 20),
    )(amplitudes, integrals)


def transpose_block(values, width):
    count = values.shape[0]
    return values.reshape(count, width, width).transpose(0, 2, 1).reshape(count, width * width)


def per_device(amplitudes, integrals, occ_pairs, partners, virt_list, eps_occ, eps_virt):
    width = virt_list.shape[0]
    mine, other = ladder_rows(amplitudes, integrals)
    flipped = jnp.take(other, partners % mine.shape[0], axis=0, mode="clip")
    total = mine + transpose_block(flipped, width)
    occ_ids = jnp.arange(eps_occ.shape[0], dtype=jnp.int32)
    occ_match = occ_pairs[:, :, None] == occ_ids[None, None, :]
    occ_sum = jnp.sum(jnp.where(occ_match, eps_occ[None, None, :], 0.0), axis=(1, 2))
    virt_ids = jnp.arange(eps_virt.shape[0], dtype=jnp.int32)
    virt_match = virt_list[:, None] == virt_ids[None, :]
    virt_energy = jnp.sum(jnp.where(virt_match, eps_virt[None, :], 0.0), axis=1)
    virt_sum = (virt_energy[:, None] + virt_energy[None, :]).reshape(-1)
    denominator = virt_sum[None, :] - occ_sum[:, None]
    return total / denominator


def solution(mesh):
    placed = (
        P("pair", "virt"),
        P("virt", "pair"),
        P(("pair", "virt"), None),
        P(("pair", "virt")),
        P(),
        P(),
        P(),
    )
    return jax.shard_map(
        per_device, mesh=mesh, in_specs=placed, out_specs=P(("pair", "virt"), None), check_vma=False
    )
```
